32 devices in a mesh: gx: 4 (over z), gy: 8 (over y, x, core).
Axes of the slice: x: 2, y: 2, z: 4, core: 2. Of those that a mesh axis runs over, the one named last changes fastest.
Arguments:
- partials: float32 [8192, 512], P(('gx', 'gy')), may hold values from -6 to 6
- partial_ids: int32 [32, 256], replicated, may hold values from 0 to 127
- read_lists: int32 [32, 1024], replicated, may hold values from 0 to 127
- sources: int32 [32, 8192], P(('gx', 'gy')), may hold values from 0 to 1023
- targets: int32 [32, 8192], P(('gx', 'gy')), may hold values from 0 to 127
- kernels: float32 [8, 512, 512], replicated, may hold values from -0.03125 to 0.03125
Outputs:
- local_expansions: float32 [4096, 512], P(('gx', 'gy'))
The draws below stay inside these ranges and needn't reach their ends.
All inputs are finite; a program needn't handle non-finite values.
Results may differ from the reference program's by a relative error of at most 0.0003.
Values sent between devices are 32-bit elements; how exact they have to be, the bound alone decides.
A program may use at most 192 MiB of HBM per device.

```python
import jax
import jax.numpy as jnp
from jax import lax

P_SIZE = 512
OCT_DEV = 128
LIST_DEV = 8192
DIRS = 8
SLOTS = 256
READS = 1024
N_GX = 4
N_GY = 8
DEVICES = 32


def set_ends(array, own_key, low, top_value):
    extent = array.shape
    spot = [jax.random.randint(jax.random.fold_in(own_key, axis), (), 0, extent[axis]) for axis in range(len(extent))]
    array = array.at[tuple(spot)].set(low)
    longest = extent.index(max(extent))
    spot[longest] = (spot[longest] + 1) % extent[longest]
    return array.at[tuple(spot)].set(top_value)


def levels(rng, dims, pieces, least, largest):
    loudness, own = 1.0, jax.random.fold_in(rng, 6)
    for position, blocks in pieces:
        heights = jnp.exp(jax.random.uniform(jax.random.fold_in(own, position), (blocks,), jnp.float32, least / len(pieces), largest / len(pieces)))
        loudness = loudness * jnp.repeat(heights, dims[position] // blocks).reshape([-1 if axis == position else 1 for axis in range(len(dims))])
    return loudness


def scatter_about(own_key, extent, scale, most, split=(), kind=jnp.bfloat16):
    entries = scale * jax.random.normal(own_key, extent, jnp.float32)
    if split:
        entries = entries * levels(own_key, extent, split, -0.22, 0.18)
    return jnp.clip(entries, -most, most).astype(kind)


def setup_inputs(seed: int = 0) -> dict:
    key_of = jax.random.split(jax.random.key(seed), 7)
    partials = scatter_about(key_of[0], (DEVICES * SLOTS, P_SIZE), ((OCT_DEV / SLOTS) ** 0.5), 6.0, ((0, 32),), jnp.float32)
    partial_ids = set_ends(jax.random.randint(key_of[1], (DEVICES, SLOTS), 0, OCT_DEV), jax.random.fold_in(key_of[1], 1), 0, OCT_DEV - 1).astype(jnp.int32)
    read_lists = set_ends(jax.random.randint(key_of[2], (DEVICES, READS), 0, OCT_DEV), jax.random.fold_in(key_of[2], 1), 0, OCT_DEV - 1).astype(jnp.int32)
    sources = set_ends(jax.random.randint(key_of[3], (DEVICES, LIST_DEV), 0, READS), jax.random.fold_in(key_of[3], 1), 0, READS - 1).astype(jnp.int32)
    targets = set_ends(jax.random.randint(key_of[4], (DEVICES, LIST_DEV), 0, OCT_DEV), jax.random.fold_in(key_of[4], 1), 0, OCT_DEV - 1).astype(jnp.int32)
    kernels = scatter_about(key_of[5], (DIRS, P_SIZE, P_SIZE), (P_SIZE * LIST_DEV // OCT_DEV) ** -0.5, 0.03125, (), jnp.float32)
    return {"partials": partials, "partial_ids": partial_ids, "read_lists": read_lists, "sources": sources, "targets": targets, "kernels": kernels}


def reference(partials, partial_ids, read_lists, sources, targets, kernels):
    devices = N_GX * N_GY
    width = partials.shape[1]
    slots = partial_ids.shape[1]
    per_owner = slots // devices
    owner_base = (jnp.arange(slots, dtype=jnp.int32) // per_owner) * OCT_DEV
    global_ids = (owner_base[None, :] + partial_ids).reshape(-1).astype(jnp.int32)
    density = jax.ops.segment_sum(partials, global_ids, num_segments=OCT_DEV * devices)
    reads = read_lists.shape[1]
    per_reader = reads // devices
    read_base = (jnp.arange(reads, dtype=jnp.int32) // per_reader) * OCT_DEV
    kernels32 = kernels.astype(jnp.float32)

    def one_reader(inputs):
        own_reads, own_sources, own_targets = inputs
        slot_global = (read_base + own_reads).astype(jnp.int32)
        entry_rows = jnp.take(density, slot_global[own_sources], axis=0)
        grouped = entry_rows.reshape(DIRS, -1, width)
        images = jnp.einsum("dkp,dqp->dkq", grouped, kernels32, precision=lax.Precision.HIGHEST)
        return jax.ops.segment_sum(images.reshape(-1, width), own_targets, num_segments=OCT_DEV)

    result = lax.map(one_reader, (read_lists, sources, targets))
    return result.reshape(-1, width)
```

```python
import functools

import jax
import jax.numpy as jnp
from jax import lax
from jax.experimental import pallas as pl
from jax.experimental.pallas import tpu as pltpu
from jax.sharding import PartitionSpec as P

OCT_DEV = 128
DIRS = 8
MESH = pl.DeviceIdType.MESH
F32 = jnp.float32
BF16 = jnp.bfloat16


def split2(x):
    hi = x.astype(BF16)
    return hi, (x - hi.astype(F32)).astype(BF16)


def onehot(mask):
    return jnp.where(mask, 1.0, 0.0).astype(F32).astype(BF16)


def dot(a, b):
    return lax.dot_general(a, b, (((1,), (0,)), ((), ())), preferred_element_type=F32)


def dot_nt(a, b):
    return lax.dot_general(a, b, (((1,), (1,)), ((), ())), preferred_element_type=F32)


def kernel(
    gxn, gyn, per_owner, per_reader,
    partials, pids, rlists, src, tgt, kern, out,
    recv, dens, outgoing, rows, chi, clo, acc, khi, klo, kbuf, wcol,
    s1, r1, l1, ksem, ag_send, ag_recv, pl_send, pl_recv,
):
    n = gxn * gyn
    gx = lax.axis_index("gx")
    gy = lax.axis_index("gy")
    me = gx * gyn + gy
    slots = n * per_owner
    half = gyn * per_reader
    per_dir = src.shape[1] // DIRS

    barrier = pltpu.get_barrier_semaphore()

    def peer(step):
        o = lax.rem(me + step, n)
        return o, (o // gyn, lax.rem(o, gyn))

    def greet(step, c):
        _, dev = peer(step)
        pl.semaphore_signal(barrier, inc=1, device_id=dev, device_id_type=MESH)
        return c

    lax.fori_loop(1, n, greet, 0)

    def kcopy(d):
        s = lax.rem(d, 2)
        return pltpu.make_async_copy(kern.at[d], kbuf.at[s], ksem.at[s])

    own = pltpu.make_async_copy(
        partials.at[pl.ds(pl.multiple_of(me * per_owner, 8), per_owner)],
        recv.at[pl.ds(pl.multiple_of(me * per_owner, 8), per_owner)],
        l1,
    )
    own.start()
    kcopy(0).start()
    kcopy(1).start()
    pl.semaphore_wait(barrier, n - 1)

    def send1(step, c):
        o, dev = peer(step)
        pltpu.make_async_remote_copy(
            src_ref=partials.at[pl.ds(pl.multiple_of(o * per_owner, 8), per_owner)],
            dst_ref=recv.at[pl.ds(pl.multiple_of(me * per_owner, 8), per_owner)],
            send_sem=s1, recv_sem=r1, device_id=dev, device_id_type=MESH,
        ).start()
        return c

    lax.fori_loop(1, n, send1, 0)

    def counts(d, c):
        at = pl.ds(pl.multiple_of(d * per_dir, 128), per_dir)
        s = src[:, at]
        t = tgt[:, at]
        h = jnp.zeros_like(s)
        for k in range(1, gxn):
            h = h + jnp.where(s >= k * half, 1, 0)
        lo = s - h * half
        comb = h * OCT_DEV + t
        tpick = onehot(lax.broadcasted_iota(jnp.int32, (gxn * OCT_DEV, per_dir), 0) == comb)
        spick = onehot(lax.broadcasted_iota(jnp.int32, (half, per_dir), 0) == lo)
        cnt = dot_nt(tpick, spick)
        hi, low = split2(cnt)
        row = pl.ds(pl.multiple_of(d * OCT_DEV, OCT_DEV), OCT_DEV)
        for k in range(gxn):
            chi[k, row, :] = hi[k * OCT_DEV:(k + 1) * OCT_DEV]
            clo[k, row, :] = low[k * OCT_DEV:(k + 1) * OCT_DEV]
        kcopy(d).wait()
        kh, kl = split2(kbuf[lax.rem(d, 2)])
        khi[d] = kh
        klo[d] = kl

        @pl.when(d + 2 < DIRS)
        def _():
            kcopy(d + 2).start()

        return c

    lax.fori_loop(0, DIRS, counts, 0)

    plane = rlists[pl.ds(pl.multiple_of(gx * gyn, 8), gyn), :].astype(F32).astype(BF16)
    c_iota = lax.broadcasted_iota(jnp.int32, (half, 1), 0)
    q_of = lax.rem(c_iota, per_reader)
    j_of = lax.div(c_iota, per_reader)
    j_mask = lax.broadcasted_iota(jnp.int32, (half, gyn), 1) == j_of
    s_iota = lax.broadcasted_iota(jnp.int32, (half, plane.shape[1]), 1)

    def picks(z, c):
        sel = onehot(s_iota == (z * gyn + gy) * per_reader + q_of)
        m = dot_nt(sel, plane)
        col = jnp.sum(jnp.where(j_mask, m, 0.0), axis=1, keepdims=True)
        wcol[z] = onehot(
            lax.broadcasted_iota(jnp.int32, (half, OCT_DEV), 1) == col.astype(jnp.int32)
        )
        return c

    lax.fori_loop(0, gxn, picks, 0)

    e_iota = lax.broadcasted_iota(jnp.int32, (1, slots), 1)
    sel = onehot(
        lax.broadcasted_iota(jnp.int32, (slots, slots), 0)
        == me * per_owner + lax.rem(e_iota, per_owner)
    )
    m = dot(pids[...].astype(F32).astype(BF16), sel)
    keep = lax.broadcasted_iota(jnp.int32, (n, slots), 0) == lax.div(e_iota, per_owner)
    ids = jnp.sum(jnp.where(keep, m, 0.0), axis=0, keepdims=True).astype(jnp.int32)
    selector = onehot(lax.broadcasted_iota(jnp.int32, (OCT_DEV, slots), 0) == ids)
    acc[...] = jnp.zeros_like(acc)

    own.wait()
    rest = recv.at[pl.ds(0, (n - 1) * per_owner)]
    all1 = pltpu.make_async_remote_copy(
        src_ref=rest, dst_ref=rest, send_sem=s1, recv_sem=r1,
        device_id=(gx, gy), device_id_type=MESH,
    )
    all1.wait_recv()
    p_hi, p_lo = split2(recv[...])
    dens[gx] = dot(selector, p_hi) + dot(selector, p_lo)

    def along(z, up):
        to = gx + 1 if up else gx - 1
        return pltpu.make_async_remote_copy(
            src_ref=dens.at[z], dst_ref=dens.at[z],
            send_sem=ag_send.at[1 if up else 0, z], recv_sem=ag_recv.at[z],
            device_id=(to, gy), device_id_type=MESH,
        )

    def spread(z):
        d_hi, d_lo = split2(dens[z])
        outgoing[z] = dot(wcol[z], d_hi) + dot(wcol[z], d_lo)
        base = pl.multiple_of(z * half + gy * per_reader, 8)

        def one(step, c):
            j = lax.rem(gy + step, gyn)
            pltpu.make_async_remote_copy(
                src_ref=outgoing.at[z, pl.ds(pl.multiple_of(j * per_reader, 8), per_reader)],
                dst_ref=rows.at[pl.ds(base, per_reader)],
                send_sem=pl_send.at[z], recv_sem=pl_recv.at[z],
                device_id=(gx, j), device_id_type=MESH,
            ).start()
            return c

        lax.fori_loop(1, gyn, one, 0)
        rows[pl.ds(base, per_reader), :] = outgoing[
            z, pl.ds(pl.multiple_of(gy * per_reader, 8), per_reader), :
        ]

    def plane_all(z):
        part = rows.at[pl.ds(0, (gyn - 1) * per_reader)]
        return pltpu.make_async_remote_copy(
            src_ref=part, dst_ref=part, send_sem=pl_send.at[z], recv_sem=pl_recv.at[z],
            device_id=(gx, gy), device_id_type=MESH,
        )

    def collect(z):
        plane_all(z).wait_recv()
        r_hi, r_lo = split2(rows[pl.ds(pl.multiple_of(z * half, 8), half), :])
        acc[...] += dot(chi[z], r_hi) + dot(chi[z], r_lo) + dot(clo[z], r_hi)

    @pl.when(gx + 1 < gxn)
    def _():
        along(gx, True).start()

    @pl.when(gx > 0)
    def _():
        along(gx, False).start()

    spread(gx)

    def place(j):
        k = j // 2 + 1
        return gx + jnp.where(lax.rem(j, 2) == 0, -k, k)

    def phase2(j, c):
        z = place(j)
        ok = (z >= 0) & (z < gxn)

        @pl.when(ok)
        def _():
            along(z, True).wait_recv()

        @pl.when(ok & (z < gx) & (gx + 1 < gxn))
        def _():
            along(z, True).start()

        @pl.when(ok & (z > gx) & (gx > 0))
        def _():
            along(z, False).start()

        @pl.when(ok)
        def _():
            spread(z)

        y = jnp.where(j == 0, gx, place(jnp.maximum(j - 1, 0)))

        @pl.when((y >= 0) & (y < gxn))
        def _():
            collect(y)

        return c

    steps = 2 * (gxn - 1)
    lax.fori_loop(0, steps, phase2, 0)
    last = place(steps - 1)

    @pl.when((last >= 0) & (last < gxn))
    def _():
        collect(last)

    out[...] = jnp.zeros_like(out)

    def final(d, c):
        c_hi, c_lo = split2(acc[pl.ds(pl.multiple_of(d * OCT_DEV, OCT_DEV), OCT_DEV), :])
        out[...] += dot_nt(c_hi, khi[d]) + dot_nt(c_lo, khi[d]) + dot_nt(c_hi, klo[d])
        return c

    lax.fori_loop(0, DIRS, final, 0)

    all1.wait_send()

    def drain(z, c):
        plane_all(z).wait_send()

        @pl.when((z <= gx) & (gx + 1 < gxn))
        def _():
            along(z, True).wait_send()

        @pl.when((z >= gx) & (gx > 0))
        def _():
            along(z, False).wait_send()

        return c

    lax.fori_loop(0, gxn, drain, 0)


def body(partials, partial_ids, read_lists, sources, targets, kernels):
    gxn = lax.axis_size("gx")
    gyn = lax.axis_size("gy")
    n = gxn * gyn
    width = partials.shape[1]
    per_owner = partials.shape[0] // n
    reads = read_lists.shape[1]
    per_reader = reads // n
    half = gyn * per_reader
    vmem = pl.BlockSpec(memory_space=pltpu.VMEM)
    hbm = pl.BlockSpec(memory_space=pl.ANY)
    dma = pltpu.SemaphoreType.DMA
    return pl.pallas_call(
        functools.partial(kernel, gxn, gyn, per_owner, per_reader),
        out_shape=jax.ShapeDtypeStruct((OCT_DEV, width), F32),
        in_specs=[hbm, vmem, vmem, vmem, vmem, hbm],
        out_specs=vmem,
        scratch_shapes=[
            pltpu.VMEM((n * per_owner, width), F32),
            pltpu.VMEM((gxn, OCT_DEV, width), F32),
            pltpu.VMEM((gxn, half, width), F32),
            pltpu.VMEM((reads, width), F32),
            pltpu.VMEM((gxn, DIRS * OCT_DEV, half), BF16),
            pltpu.VMEM((gxn, DIRS * OCT_DEV, half), BF16),
            pltpu.VMEM((DIRS * OCT_DEV, width), F32),
            pltpu.VMEM((DIRS, width, width), BF16),
            pltpu.VMEM((DIRS, width, width), BF16),
            pltpu.VMEM((2, width, width), F32),
            pltpu.VMEM((gxn, half, OCT_DEV), BF16),
            dma, dma, dma, dma((2,)), dma((2, gxn)), dma((gxn,)), dma((gxn,)), dma((gxn,)),
        ],
        compiler_params=pltpu.CompilerParams(
            collective_id=0, has_side_effects=True, vmem_limit_bytes=62 * 1024 * 1024
        ),
    )(partials, partial_ids, read_lists, sources, targets, kernels)


def solution(mesh):
    return jax.shard_map(
        body,
        mesh=mesh,
        in_specs=(
            P(("gx", "gy"), None),
            P(),
            P(),
            P(("gx", "gy"), None),
            P(("gx", "gy"), None),
            P(),
        ),
        out_specs=P(("gx", "gy"), None),
        check_vma=False,
    )
```

```python
import functools

import jax
import jax.numpy as jnp
from jax import lax
from jax.experimental import pallas as pl
from jax.experimental.pallas import tpu as pltpu
from jax.sharding import PartitionSpec as P

OCT_DEV = 128
DIRS = 8
MESH = pl.DeviceIdType.MESH
F32 = jnp.float32
BF16 = jnp.bfloat16


def split2(x):
    hi = x.astype(BF16)
    return hi, (x - hi.astype(F32)).astype(BF16)


def onehot(mask):
    return jnp.where(mask, 1.0, 0.0).astype(F32).astype(BF16)


def dot(a, b):
    return lax.dot_general(a, b, (((1,), (0,)), ((), ())), preferred_element_type=F32)


def dot_nt(a, b):
    return lax.dot_general(a, b, (((1,), (1,)), ((), ())), preferred_element_type=F32)


def partner(i, k):
    bit = 1
    while bit <= k:
        if k & bit:
            i = i + bit - 2 * bit * lax.rem(i // bit, 2)
        bit *= 2
    return i


def kernel(
    gxn, gyn, per_owner, per_reader,
    partials, pids, rlists, src, tgt, kern, out,
    recv, dens, outgoing, rows, chi, clo, acc, khi, klo, kbuf, wcol,
    s1, r1, l1, ksem, ag_send, ag_recv, pl_send, pl_recv,
):
    n = gxn * gyn
    gx = lax.axis_index("gx")
    gy = lax.axis_index("gy")
    me = gx * gyn + gy
    slots = n * per_owner
    half = gyn * per_reader
    per_dir = src.shape[1] // DIRS

    order = sorted(range(1, gyn), key=lambda k: (bin(k >> 1).count("1") or gyn, k & 1, k))
    barrier = pltpu.get_barrier_semaphore()

    def peer(step):
        o = lax.rem(me + step, n)
        return o, (o // gyn, lax.rem(o, gyn))

    def greet(step, c):
        _, dev = peer(step)
        pl.semaphore_signal(barrier, inc=1, device_id=dev, device_id_type=MESH)
        return c

    lax.fori_loop(1, n, greet, 0)

    def kcopy(d):
        s = lax.rem(d, 2)
        return pltpu.make_async_copy(kern.at[d], kbuf.at[s], ksem.at[s])

    own = pltpu.make_async_copy(
        partials.at[pl.ds(pl.multiple_of(me * per_owner, 8), per_owner)],
        recv.at[pl.ds(pl.multiple_of(me * per_owner, 8), per_owner)],
        l1,
    )
    own.start()
    kcopy(0).start()
    kcopy(1).start()
    pl.semaphore_wait(barrier, n - 1)

    def send1(step, c):
        o, dev = peer(step)
        pltpu.make_async_remote_copy(
            src_ref=partials.at[pl.ds(pl.multiple_of(o * per_owner, 8), per_owner)],
            dst_ref=recv.at[pl.ds(pl.multiple_of(me * per_owner, 8), per_owner)],
            send_sem=s1, recv_sem=r1, device_id=dev, device_id_type=MESH,
        ).start()
        return c

    lax.fori_loop(1, n, send1, 0)

    def counts(d, c):
        at = pl.ds(pl.multiple_of(d * per_dir, 128), per_dir)
        s = src[:, at]
        t = tgt[:, at]
        h = jnp.zeros_like(s)
        for k in range(1, gxn):
            h = h + jnp.where(s >= k * half, 1, 0)
        lo = s - h * half
        comb = h * OCT_DEV + t
        tpick = onehot(lax.broadcasted_iota(jnp.int32, (gxn * OCT_DEV, per_dir), 0) == comb)
        spick = onehot(lax.broadcasted_iota(jnp.int32, (half, per_dir), 0) == lo)
        cnt = dot_nt(tpick, spick)
        hi, low = split2(cnt)
        row = pl.ds(pl.multiple_of(d * OCT_DEV, OCT_DEV), OCT_DEV)
        for k in range(gxn):
            chi[k, row, :] = hi[k * OCT_DEV:(k + 1) * OCT_DEV]
            clo[k, row, :] = low[k * OCT_DEV:(k + 1) * OCT_DEV]
        kcopy(d).wait()
        kh, kl = split2(kbuf[lax.rem(d, 2)])
        khi[d] = kh
        klo[d] = kl

        @pl.when(d + 2 < DIRS)
        def _():
            kcopy(d + 2).start()

        return c

    lax.fori_loop(0, DIRS, counts, 0)

    plane = rlists[pl.ds(pl.multiple_of(gx * gyn, 8), gyn), :].astype(F32).astype(BF16)
    c_iota = lax.broadcasted_iota(jnp.int32, (half, 1), 0)
    q_of = lax.rem(c_iota, per_reader)
    j_of = lax.div(c_iota, per_reader)
    j_mask = lax.broadcasted_iota(jnp.int32, (half, gyn), 1) == j_of
    s_iota = lax.broadcasted_iota(jnp.int32, (half, plane.shape[1]), 1)

    def picks(z, c):
        sel = onehot(s_iota == (z * gyn + gy) * per_reader + q_of)
        m = dot_nt(sel, plane)
        col = jnp.sum(jnp.where(j_mask, m, 0.0), axis=1, keepdims=True)
        wcol[z] = onehot(
            lax.broadcasted_iota(jnp.int32, (half, OCT_DEV), 1) == col.astype(jnp.int32)
        )
        return c

    lax.fori_loop(0, gxn, picks, 0)

    e_iota = lax.broadcasted_iota(jnp.int32, (1, slots), 1)
    sel = onehot(
        lax.broadcasted_iota(jnp.int32, (slots, slots), 0)
        == me * per_owner + lax.rem(e_iota, per_owner)
    )
    m = dot(pids[...].astype(F32).astype(BF16), sel)
    keep = lax.broadcasted_iota(jnp.int32, (n, slots), 0) == lax.div(e_iota, per_owner)
    ids = jnp.sum(jnp.where(keep, m, 0.0), axis=0, keepdims=True).astype(jnp.int32)
    selector = onehot(lax.broadcasted_iota(jnp.int32, (OCT_DEV, slots), 0) == ids)
    acc[...] = jnp.zeros_like(acc)

    own.wait()
    rest = recv.at[pl.ds(0, (n - 1) * per_owner)]
    all1 = pltpu.make_async_remote_copy(
        src_ref=rest, dst_ref=rest, send_sem=s1, recv_sem=r1,
        device_id=(gx, gy), device_id_type=MESH,
    )
    all1.wait_recv()
    p_hi, p_lo = split2(recv[...])
    dens[gx] = dot(selector, p_hi) + dot(selector, p_lo)

    def along(z, up):
        to = gx + 1 if up else gx - 1
        return pltpu.make_async_remote_copy(
            src_ref=dens.at[z], dst_ref=dens.at[z],
            send_sem=ag_send.at[1 if up else 0, z], recv_sem=ag_recv.at[z],
            device_id=(to, gy), device_id_type=MESH,
        )

    def spread(z):
        d_hi, d_lo = split2(dens[z])
        outgoing[z] = dot(wcol[z], d_hi) + dot(wcol[z], d_lo)
        base = pl.multiple_of(z * half + gy * per_reader, 8)

        for k in order:
            j = partner(gy, k)
            pltpu.make_async_remote_copy(
                src_ref=outgoing.at[z, pl.ds(pl.multiple_of(j * per_reader, 8), per_reader)],
                dst_ref=rows.at[pl.ds(base, per_reader)],
                send_sem=pl_send.at[z], recv_sem=pl_recv.at[z],
                device_id=(gx, j), device_id_type=MESH,
            ).start()
        rows[pl.ds(base, per_reader), :] = outgoing[
            z, pl.ds(pl.multiple_of(gy * per_reader, 8), per_reader), :
        ]

    def plane_all(z):
        part = rows.at[pl.ds(0, (gyn - 1) * per_reader)]
        return pltpu.make_async_remote_copy(
            src_ref=part, dst_ref=part, send_sem=pl_send.at[z], recv_sem=pl_recv.at[z],
            device_id=(gx, gy), device_id_type=MESH,
        )

    def collect(z):
        plane_all(z).wait_recv()
        r_hi, r_lo = split2(rows[pl.ds(pl.multiple_of(z * half, 8), half), :])
        c_hi = chi[z]
        acc[...] += dot(
            jnp.concatenate([c_hi, c_hi, clo[z]], axis=1),
            jnp.concatenate([r_hi, r_lo, r_hi], axis=0),
        )

    @pl.when(gx + 1 < gxn)
    def _():
        along(gx, True).start()

    @pl.when(gx > 0)
    def _():
        along(gx, False).start()

    spread(gx)

    def inside(z):
        return (z >= 0) & (z < gxn)

    def level(k, c):
        low = gx - k
        high = gx + k

        @pl.when(inside(low))
        def _():
            along(low, True).wait_recv()

        @pl.when(inside(low) & (gx + 1 < gxn))
        def _():
            along(low, True).start()

        @pl.when(inside(high))
        def _():
            along(high, False).wait_recv()

        @pl.when(inside(high) & (gx > 0))
        def _():
            along(high, False).start()

        def side(i, c):
            z = gx + (2 * i - 1) * k

            @pl.when(inside(z))
            def _():
                spread(z)

            return c

        lax.fori_loop(0, 2, side, 0)

        def back(i, c):
            z = gx + (2 * i - 1) * (k - 1)

            @pl.when(inside(z) & ((k > 1) | (i == 0)))
            def _():
                collect(z)

            return c

        lax.fori_loop(0, 2, back, 0)
        return c

    lax.fori_loop(1, gxn, level, 0)

    def rest_of(i, c):
        z = gx + (2 * i - 1) * (gxn - 1)

        @pl.when(inside(z))
        def _():
            collect(z)

        return c

    lax.fori_loop(0, 2, rest_of, 0)
    out[...] = jnp.zeros_like(out)

    def final(d, c):
        c_hi, c_lo = split2(acc[pl.ds(pl.multiple_of(d * OCT_DEV, OCT_DEV), OCT_DEV), :])
        both = dot_nt(jnp.concatenate([c_hi, c_lo], axis=0), khi[d])
        out[...] += both[:OCT_DEV] + both[OCT_DEV:] + dot_nt(c_hi, klo[d])
        return c

    lax.fori_loop(0, DIRS, final, 0)

    all1.wait_send()

    def drain(z, c):
        plane_all(z).wait_send()

        @pl.when((z <= gx) & (gx + 1 < gxn))
        def _():
            along(z, True).wait_send()

        @pl.when((z >= gx) & (gx > 0))
        def _():
            along(z, False).wait_send()

        return c

    lax.fori_loop(0, gxn, drain, 0)


def body(partials, partial_ids, read_lists, sources, targets, kernels):
    gxn = lax.axis_size("gx")
    gyn = lax.axis_size("gy")
    n = gxn * gyn
    width = partials.shape[1]
    per_owner = partials.shape[0] // n
    reads = read_lists.shape[1]
    per_reader = reads // n
    half = gyn * per_reader
    vmem = pl.BlockSpec(memory_space=pltpu.VMEM)
    hbm = pl.BlockSpec(memory_space=pl.ANY)
    dma = pltpu.SemaphoreType.DMA
    return pl.pallas_call(
        functools.partial(kernel, gxn, gyn, per_owner, per_reader),
        out_shape=jax.ShapeDtypeStruct((OCT_DEV, width), F32),
        in_specs=[hbm, vmem, vmem, vmem, vmem, hbm],
        out_specs=vmem,
        scratch_shapes=[
            pltpu.VMEM((n * per_owner, width), F32),
            pltpu.VMEM((gxn, OCT_DEV, width), F32),
            pltpu.VMEM((gxn, half, width), F32),
            pltpu.VMEM((reads, width), F32),
            pltpu.VMEM((gxn, DIRS * OCT_DEV, half), BF16),
            pltpu.VMEM((gxn, DIRS * OCT_DEV, half), BF16),
            pltpu.VMEM((DIRS * OCT_DEV, width), F32),
            pltpu.VMEM((DIRS, width, width), BF16),
            pltpu.VMEM((DIRS, width, width), BF16),
            pltpu.VMEM((2, width, width), F32),
            pltpu.VMEM((gxn, half, OCT_DEV), BF16),
            dma, dma, dma, dma((2,)), dma((2, gxn)), dma((gxn,)), dma((gxn,)), dma((gxn,)),
        ],
        compiler_params=pltpu.CompilerParams(
            collective_id=0, has_side_effects=True, vmem_limit_bytes=62 * 1024 * 1024
        ),
    )(partials, partial_ids, read_lists, sources, targets, kernels)


def solution(mesh):
    return jax.shard_map(
        body,
        mesh=mesh,
        in_specs=(
            P(("gx", "gy"), None),
            P(),
            P(),
            P(("gx", "gy"), None),
            P(("gx", "gy"), None),
            P(),
        ),
        out_specs=P(("gx", "gy"), None),
        check_vma=False,
    )
```

```python
import functools

import jax
import jax.numpy as jnp
from jax import lax
from jax.experimental import pallas as pl
from jax.experimental.pallas import tpu as pltpu
from jax.sharding import PartitionSpec as P

OCT_DEV = 128
DIRS = 8
MESH = pl.DeviceIdType.MESH
F32 = jnp.float32
BF16 = jnp.bfloat16


def split2(x):
    hi = x.astype(BF16)
    return hi, (x - hi.astype(F32)).astype(BF16)


def onehot(mask):
    return jnp.where(mask, 1.0, 0.0).astype(F32).astype(BF16)


def dot(a, b):
    return lax.dot_general(a, b, (((1,), (0,)), ((), ())), preferred_element_type=F32)


def dot_nt(a, b):
    return lax.dot_general(a, b, (((1,), (1,)), ((), ())), preferred_element_type=F32)


def partner(i, k):
    bit = 1
    while bit <= k:
        if k & bit:
            i = i + bit - 2 * bit * lax.rem(i // bit, 2)
        bit *= 2
    return i


def kernel(
    gxn, gyn, per_owner, per_reader,
    partials, pids_hbm, rlists_hbm, src_hbm, tgt_hbm, kern, out,
    recv, dens, outgoing, rows, chi, clo, acc, khi, klo, kbuf, wcol, pids, rlists, src, tgt,
    s1, r1, l1, isem, ksem, ag_send, ag_recv, pl_send, pl_recv,
):
    n = gxn * gyn
    gx = lax.axis_index("gx")
    gy = lax.axis_index("gy")
    me = gx * gyn + gy
    slots = n * per_owner
    half = gyn * per_reader
    per_dir = src.shape[1] // DIRS
    width = partials.shape[1] // 2

    order = sorted(range(1, gyn), key=lambda k: (bin(k >> 1).count("1") or gyn, k & 1, k))
    barrier = pltpu.get_barrier_semaphore()
    loads = [
        pltpu.make_async_copy(a, b, isem.at[i])
        for i, (a, b) in enumerate(
            ((src_hbm, src), (tgt_hbm, tgt), (rlists_hbm, rlists), (pids_hbm, pids))
        )
    ]

    def peer(step):
        o = lax.rem(me + step, n)
        return o, (o // gyn, lax.rem(o, gyn))

    def greet(step, c):
        _, dev = peer(step)
        pl.semaphore_signal(barrier, inc=1, device_id=dev, device_id_type=MESH)
        return c

    lax.fori_loop(1, n, greet, 0)

    def kcopy(d):
        s = lax.rem(d, 2)
        return pltpu.make_async_copy(kern.at[d], kbuf.at[s], ksem.at[s])

    own = pltpu.make_async_copy(
        partials.at[pl.ds(pl.multiple_of(me * per_owner, 8), per_owner)],
        recv.at[pl.ds(pl.multiple_of(me * per_owner, 8), per_owner)],
        l1,
    )
    own.start()
    for load in loads:
        load.start()
    kcopy(0).start()
    kcopy(1).start()
    pl.semaphore_wait(barrier, n - 1)

    def send1(step, c):
        o, dev = peer(step)
        pltpu.make_async_remote_copy(
            src_ref=partials.at[pl.ds(pl.multiple_of(o * per_owner, 8), per_owner)],
            dst_ref=recv.at[pl.ds(pl.multiple_of(me * per_owner, 8), per_owner)],
            send_sem=s1, recv_sem=r1, device_id=dev, device_id_type=MESH,
        ).start()
        return c

    lax.fori_loop(1, n, send1, 0)

    for load in loads:
        load.wait()

    def counts(d, c):
        at = pl.ds(pl.multiple_of(d * per_dir, 128), per_dir)
        s = src[:, at]
        t = tgt[:, at]
        h = jnp.zeros_like(s)
        for k in range(1, gxn):
            h = h + jnp.where(s >= k * half, 1, 0)
        lo = s - h * half
        comb = h * OCT_DEV + t
        tpick = onehot(lax.broadcasted_iota(jnp.int32, (gxn * OCT_DEV, per_dir), 0) == comb)
        spick = onehot(lax.broadcasted_iota(jnp.int32, (half, per_dir), 0) == lo)
        cnt = dot_nt(tpick, spick)
        hi, low = split2(cnt)
        row = pl.ds(pl.multiple_of(d * OCT_DEV, OCT_DEV), OCT_DEV)
        for k in range(gxn):
            chi[k, row, :] = hi[k * OCT_DEV:(k + 1) * OCT_DEV]
            clo[k, row, :] = low[k * OCT_DEV:(k + 1) * OCT_DEV]
        kcopy(d).wait()
        kh, kl = split2(kbuf[lax.rem(d, 2)])
        khi[d] = kh
        klo[d] = kl

        @pl.when(d + 2 < DIRS)
        def _():
            kcopy(d + 2).start()

        return c

    lax.fori_loop(0, DIRS, counts, 0)

    plane = rlists[pl.ds(pl.multiple_of(gx * gyn, 8), gyn), :].astype(F32).astype(BF16)
    c_iota = lax.broadcasted_iota(jnp.int32, (half, 1), 0)
    q_of = lax.rem(c_iota, per_reader)
    j_of = lax.div(c_iota, per_reader)
    j_mask = lax.broadcasted_iota(jnp.int32, (half, gyn), 1) == j_of
    s_iota = lax.broadcasted_iota(jnp.int32, (half, plane.shape[1]), 1)

    def picks(z, c):
        sel = onehot(s_iota == (z * gyn + gy) * per_reader + q_of)
        m = dot_nt(sel, plane)
        col = jnp.sum(jnp.where(j_mask, m, 0.0), axis=1, keepdims=True)
        wcol[z] = onehot(
            lax.broadcasted_iota(jnp.int32, (half, OCT_DEV), 1) == col.astype(jnp.int32)
        )
        return c

    lax.fori_loop(0, gxn, picks, 0)

    e_iota = lax.broadcasted_iota(jnp.int32, (1, slots), 1)
    sel = onehot(
        lax.broadcasted_iota(jnp.int32, (slots, slots), 0)
        == me * per_owner + lax.rem(e_iota, per_owner)
    )
    m = dot(pids[...].astype(F32).astype(BF16), sel)
    keep = lax.broadcasted_iota(jnp.int32, (n, slots), 0) == lax.div(e_iota, per_owner)
    ids = jnp.sum(jnp.where(keep, m, 0.0), axis=0, keepdims=True).astype(jnp.int32)
    selector = onehot(lax.broadcasted_iota(jnp.int32, (OCT_DEV, slots), 0) == ids)
    acc[...] = jnp.zeros_like(acc)

    own.wait()
    rest = recv.at[pl.ds(0, (n - 1) * per_owner)]
    all1 = pltpu.make_async_remote_copy(
        src_ref=rest, dst_ref=rest, send_sem=s1, recv_sem=r1,
        device_id=(gx, gy), device_id_type=MESH,
    )
    all1.wait_recv()
    p_hi, p_lo = split2(recv[...])

    def along(z, up, f):
        to = gx + 1 if up else gx - 1
        return pltpu.make_async_remote_copy(
            src_ref=dens.at[z, f], dst_ref=dens.at[z, f],
            send_sem=ag_send.at[1 if up else 0, f, z], recv_sem=ag_recv.at[f, z],
            device_id=(to, gy), device_id_type=MESH,
        )

    def spread(z, f):
        d_hi, d_lo = split2(dens[z, f])
        outgoing[z, f] = dot(wcol[z], d_hi) + dot(wcol[z], d_lo)
        base = pl.multiple_of(z * half + gy * per_reader, 8)
        for k in order:
            j = partner(gy, k)
            pltpu.make_async_remote_copy(
                src_ref=outgoing.at[z, f, pl.ds(pl.multiple_of(j * per_reader, 8), per_reader)],
                dst_ref=rows.at[f, pl.ds(base, per_reader)],
                send_sem=pl_send.at[f, z], recv_sem=pl_recv.at[f, z],
                device_id=(gx, j), device_id_type=MESH,
            ).start()
        rows[f, pl.ds(base, per_reader), :] = outgoing[
            z, f, pl.ds(pl.multiple_of(gy * per_reader, 8), per_reader), :
        ]

    def plane_all(z, f):
        part = rows.at[f, pl.ds(0, (gyn - 1) * per_reader)]
        return pltpu.make_async_remote_copy(
            src_ref=part, dst_ref=part, send_sem=pl_send.at[f, z], recv_sem=pl_recv.at[f, z],
            device_id=(gx, gy), device_id_type=MESH,
        )

    def collect(z, f):
        plane_all(z, f).wait_recv()
        r_hi, r_lo = split2(rows[f, pl.ds(pl.multiple_of(z * half, 8), half), :])
        c_hi = chi[z]
        acc[f] += dot(
            jnp.concatenate([c_hi, c_hi, clo[z]], axis=1),
            jnp.concatenate([r_hi, r_lo, r_hi], axis=0),
        )

    for f in range(2):
        at = slice(f * width, (f + 1) * width)
        dens[gx, f] = dot(selector, p_hi[:, at]) + dot(selector, p_lo[:, at])

        @pl.when(gx + 1 < gxn)
        def _():
            along(gx, True, f).start()

        @pl.when(gx > 0)
        def _():
            along(gx, False, f).start()

        spread(gx, f)

    def inside(z):
        return (z >= 0) & (z < gxn)

    last = jnp.where(2 * gx < gxn, gxn - 1, 0)

    def back(k):
        def one(i, c):
            z = gx + (2 * i - 1) * k

            @pl.when(inside(z) & (z != last) & ((k > 0) | (i == 0)))
            def _():
                for f in range(2):
                    collect(z, f)

            return c

        lax.fori_loop(0, 2, one, 0)

    def level(k, c):
        low = gx - k
        high = gx + k

        def part(f, c):
            @pl.when(inside(low))
            def _():
                along(low, True, f).wait_recv()

            @pl.when(inside(low) & (gx + 1 < gxn))
            def _():
                along(low, True, f).start()

            @pl.when(inside(high))
            def _():
                along(high, False, f).wait_recv()

            @pl.when(inside(high) & (gx > 0))
            def _():
                along(high, False, f).start()

            def side(i, c):
                z = gx + (2 * i - 1) * k

                @pl.when(inside(z))
                def _():
                    spread(z, f)

                return c

            lax.fori_loop(0, 2, side, 0)
            return c

        lax.fori_loop(0, 2, part, 0)

        @pl.when(k > 1)
        def _():
            back(k - 2)

        return c

    lax.fori_loop(1, gxn, level, 0)
    back(gxn - 2)
    out[...] = jnp.zeros_like(out)

    for f in range(2):
        collect(last, f)
        at = slice(f * width, (f + 1) * width)

        def final(d, c):
            c_hi, c_lo = split2(acc[f, pl.ds(pl.multiple_of(d * OCT_DEV, OCT_DEV), OCT_DEV), :])
            both = dot_nt(jnp.concatenate([c_hi, c_lo], axis=0), khi[d, :, at])
            out[...] += both[:OCT_DEV] + both[OCT_DEV:] + dot_nt(c_hi, klo[d, :, at])
            return c

        lax.fori_loop(0, DIRS, final, 0)

    all1.wait_send()

    def drain(z, c):
        for f in range(2):
            plane_all(z, f).wait_send()

            @pl.when((z <= gx) & (gx + 1 < gxn))
            def _():
                along(z, True, f).wait_send()

            @pl.when((z >= gx) & (gx > 0))
            def _():
                along(z, False, f).wait_send()

        return c

    lax.fori_loop(0, gxn, drain, 0)


def body(partials, partial_ids, read_lists, sources, targets, kernels):
    gxn = lax.axis_size("gx")
    gyn = lax.axis_size("gy")
    n = gxn * gyn
    width = partials.shape[1]
    per_owner = partials.shape[0] // n
    reads = read_lists.shape[1]
    per_reader = reads // n
    half = gyn * per_reader
    vmem = pl.BlockSpec(memory_space=pltpu.VMEM)
    hbm = pl.BlockSpec(memory_space=pl.ANY)
    dma = pltpu.SemaphoreType.DMA
    return pl.pallas_call(
        functools.partial(kernel, gxn, gyn, per_owner, per_reader),
        out_shape=jax.ShapeDtypeStruct((OCT_DEV, width), F32),
        in_specs=[hbm] * 6,
        out_specs=vmem,
        scratch_shapes=[
            pltpu.VMEM((n * per_owner, width), F32),
            pltpu.VMEM((gxn, 2, OCT_DEV, width // 2), F32),
            pltpu.VMEM((gxn, 2, half, width // 2), F32),
            pltpu.VMEM((2, reads, width // 2), F32),
            pltpu.VMEM((gxn, DIRS * OCT_DEV, half), BF16),
            pltpu.VMEM((gxn, DIRS * OCT_DEV, half), BF16),
            pltpu.VMEM((2, DIRS * OCT_DEV, width // 2), F32),
            pltpu.VMEM((DIRS, width, width), BF16),
            pltpu.VMEM((DIRS, width, width), BF16),
            pltpu.VMEM((2, width, width), F32),
            pltpu.VMEM((gxn, half, OCT_DEV), BF16),
            pltpu.VMEM(partial_ids.shape, jnp.int32),
            pltpu.VMEM(read_lists.shape, jnp.int32),
            pltpu.VMEM(sources.shape, jnp.int32),
            pltpu.VMEM(targets.shape, jnp.int32),
            dma, dma, dma, dma((4,)), dma((2,)),
            dma((2, 2, gxn)), dma((2, gxn)), dma((2, gxn)), dma((2, gxn)),
        ],
        compiler_params=pltpu.CompilerParams(
            collective_id=0, has_side_effects=True, vmem_limit_bytes=62 * 1024 * 1024
        ),
    )(partials, partial_ids, read_lists, sources, targets, kernels)


def solution(mesh):
    return jax.shard_map(
        body,
        mesh=mesh,
        in_specs=(
            P(("gx", "gy"), None),
            P(),
            P(),
            P(("gx", "gy"), None),
            P(("gx", "gy"), None),
            P(),
        ),
        out_specs=P(("gx", "gy"), None),
        check_vma=False,
    )
```

```python
import functools

import jax
import jax.numpy as jnp
from jax import lax
from jax.experimental import pallas as pl
from jax.experimental.pallas import tpu as pltpu
from jax.sharding import PartitionSpec as P

OCT_DEV = 128
DIRS = 8
MESH = pl.DeviceIdType.MESH
F32 = jnp.float32
BF16 = jnp.bfloat16


def split2(x):
    hi = x.astype(BF16)
    return hi, (x - hi.astype(F32)).astype(BF16)


def onehot(mask):
    return jnp.where(mask, 1.0, 0.0).astype(F32).astype(BF16)


def dot(a, b):
    return lax.dot_general(a, b, (((1,), (0,)), ((), ())), preferred_element_type=F32)


def dot_nt(a, b):
    return lax.dot_general(a, b, (((1,), (1,)), ((), ())), preferred_element_type=F32)


def partner(i, k):
    bit = 1
    while bit <= k:
        if k & bit:
            i = i + bit - 2 * bit * lax.rem(i // bit, 2)
        bit *= 2
    return i


def kernel(
    gxn, gyn, per_owner, per_reader,
    partials, pids_hbm, rlists_hbm, src_hbm, tgt_hbm, kern, out,
    recv, dens, outgoing, rows, chi, clo, acc, khi, klo, kbuf, wcol, pids, rlists, src, tgt,
    s1, r1, l1, isem, ksem, ag_send, ag_recv, pl_send, pl_recv,
):
    n = gxn * gyn
    gx = lax.axis_index("gx")
    gy = lax.axis_index("gy")
    me = gx * gyn + gy
    slots = n * per_owner
    half = gyn * per_reader
    per_dir = src.shape[1] // DIRS
    width = partials.shape[1] // 2

    order = sorted(range(1, gyn), key=lambda k: (bin(k >> 1).count("1") or gyn, k & 1, k))
    barrier = pltpu.get_barrier_semaphore()
    loads = [
        pltpu.make_async_copy(a, b, isem.at[i])
        for i, (a, b) in enumerate(
            ((src_hbm, src), (tgt_hbm, tgt), (rlists_hbm, rlists), (pids_hbm, pids))
        )
    ]

    def peer(step):
        o = lax.rem(me + step, n)
        return o, (o // gyn, lax.rem(o, gyn))

    def greet(step, c):
        _, dev = peer(step)
        pl.semaphore_signal(barrier, inc=1, device_id=dev, device_id_type=MESH)
        return c

    lax.fori_loop(1, n, greet, 0)

    def kcopy(d):
        s = lax.rem(d, 2)
        return pltpu.make_async_copy(kern.at[d], kbuf.at[s], ksem.at[s])

    own = pltpu.make_async_copy(
        partials.at[pl.ds(pl.multiple_of(me * per_owner, 8), per_owner)],
        recv.at[pl.ds(pl.multiple_of(me * per_owner, 8), per_owner)],
        l1,
    )
    own.start()
    for load in loads:
        load.start()
    kcopy(0).start()
    kcopy(1).start()
    pl.semaphore_wait(barrier, n - 1)

    def send1(step, c):
        o, dev = peer(step)
        pltpu.make_async_remote_copy(
            src_ref=partials.at[pl.ds(pl.multiple_of(o * per_owner, 8), per_owner)],
            dst_ref=recv.at[pl.ds(pl.multiple_of(me * per_owner, 8), per_owner)],
            send_sem=s1, recv_sem=r1, device_id=dev, device_id_type=MESH,
        ).start()
        return c

    lax.fori_loop(1, n, send1, 0)

    for load in loads:
        load.wait()

    def counts(d, c):
        at = pl.ds(pl.multiple_of(d * per_dir, 128), per_dir)
        s = src[:, at]
        t = tgt[:, at]
        h = jnp.zeros_like(s)
        for k in range(1, gxn):
            h = h + jnp.where(s >= k * half, 1, 0)
        lo = s - h * half
        comb = h * OCT_DEV + t
        tpick = onehot(lax.broadcasted_iota(jnp.int32, (gxn * OCT_DEV, per_dir), 0) == comb)
        spick = onehot(lax.broadcasted_iota(jnp.int32, (half, per_dir), 0) == lo)
        cnt = dot_nt(tpick, spick)
        hi, low = split2(cnt)
        row = pl.ds(pl.multiple_of(d * OCT_DEV, OCT_DEV), OCT_DEV)
        for k in range(gxn):
            chi[k, row, :] = hi[k * OCT_DEV:(k + 1) * OCT_DEV]
            clo[k, row, :] = low[k * OCT_DEV:(k + 1) * OCT_DEV]
        kcopy(d).wait()
        kh, kl = split2(kbuf[lax.rem(d, 2)])
        khi[d] = kh
        klo[d] = kl

        @pl.when(d + 2 < DIRS)
        def _():
            kcopy(d + 2).start()

        return c

    lax.fori_loop(0, DIRS, counts, 0)

    plane = rlists[pl.ds(pl.multiple_of(gx * gyn, 8), gyn), :].astype(F32).astype(BF16)
    c_iota = lax.broadcasted_iota(jnp.int32, (half, 1), 0)
    q_of = lax.rem(c_iota, per_reader)
    j_of = lax.div(c_iota, per_reader)
    j_mask = lax.broadcasted_iota(jnp.int32, (half, gyn), 1) == j_of
    s_iota = lax.broadcasted_iota(jnp.int32, (half, plane.shape[1]), 1)

    def picks(z, c):
        sel = onehot(s_iota == (z * gyn + gy) * per_reader + q_of)
        m = dot_nt(sel, plane)
        col = jnp.sum(jnp.where(j_mask, m, 0.0), axis=1, keepdims=True)
        wcol[z] = onehot(
            lax.broadcasted_iota(jnp.int32, (half, OCT_DEV), 1) == col.astype(jnp.int32)
        )
        return c

    lax.fori_loop(0, gxn, picks, 0)

    e_iota = lax.broadcasted_iota(jnp.int32, (1, slots), 1)
    sel = onehot(
        lax.broadcasted_iota(jnp.int32, (slots, slots), 0)
        == me * per_owner + lax.rem(e_iota, per_owner)
    )
    m = dot(pids[...].astype(F32).astype(BF16), sel)
    keep = lax.broadcasted_iota(jnp.int32, (n, slots), 0) == lax.div(e_iota, per_owner)
    ids = jnp.sum(jnp.where(keep, m, 0.0), axis=0, keepdims=True).astype(jnp.int32)
    selector = onehot(lax.broadcasted_iota(jnp.int32, (OCT_DEV, slots), 0) == ids)
    acc[...] = jnp.zeros_like(acc)

    own.wait()
    rest = recv.at[pl.ds(0, (n - 1) * per_owner)]
    all1 = pltpu.make_async_remote_copy(
        src_ref=rest, dst_ref=rest, send_sem=s1, recv_sem=r1,
        device_id=(gx, gy), device_id_type=MESH,
    )
    all1.wait_recv()
    p_hi, p_lo = split2(recv[...])

    def along(z, up, f):
        to = gx + 1 if up else gx - 1
        return pltpu.make_async_remote_copy(
            src_ref=dens.at[z, f], dst_ref=dens.at[z, f],
            send_sem=ag_send.at[1 if up else 0, f, z], recv_sem=ag_recv.at[f, z],
            device_id=(to, gy), device_id_type=MESH,
        )

    def spread(z, f):
        d_hi, d_lo = split2(dens[z, f])
        outgoing[z, f] = dot(wcol[z], d_hi) + dot(wcol[z], d_lo)
        base = pl.multiple_of(z * half + gy * per_reader, 8)
        for k in order:
            j = partner(gy, k)
            pltpu.make_async_remote_copy(
                src_ref=outgoing.at[z, f, pl.ds(pl.multiple_of(j * per_reader, 8), per_reader)],
                dst_ref=rows.at[f, pl.ds(base, per_reader)],
                send_sem=pl_send.at[f, z], recv_sem=pl_recv.at[f, z],
                device_id=(gx, j), device_id_type=MESH,
            ).start()
        rows[f, pl.ds(base, per_reader), :] = outgoing[
            z, f, pl.ds(pl.multiple_of(gy * per_reader, 8), per_reader), :
        ]

    def plane_all(z, f):
        part = rows.at[f, pl.ds(0, (gyn - 1) * per_reader)]
        return pltpu.make_async_remote_copy(
            src_ref=part, dst_ref=part, send_sem=pl_send.at[f, z], recv_sem=pl_recv.at[f, z],
            device_id=(gx, gy), device_id_type=MESH,
        )

    def collect(z, f):
        plane_all(z, f).wait_recv()
        r_hi, r_lo = split2(rows[f, pl.ds(pl.multiple_of(z * half, 8), half), :])
        c_hi = chi[z]
        acc[f] += dot(
            jnp.concatenate([c_hi, c_hi, clo[z]], axis=1),
            jnp.concatenate([r_hi, r_lo, r_hi], axis=0),
        )

    for f in range(2):
        at = slice(f * width, (f + 1) * width)
        dens[gx, f] = dot(selector, p_hi[:, at]) + dot(selector, p_lo[:, at])

        @pl.when(gx + 1 < gxn)
        def _():
            along(gx, True, f).start()

        @pl.when(gx > 0)
        def _():
            along(gx, False, f).start()

        spread(gx, f)

    def inside(z):
        return (z >= 0) & (z < gxn)

    last = jnp.where(2 * gx < gxn, gxn - 1, 0)

    def back(k):
        def one(i, c):
            z = gx + (2 * i - 1) * k

            @pl.when(inside(z) & (z != last) & ((k > 0) | (i == 0)))
            def _():
                for f in range(2):
                    collect(z, f)

            return c

        lax.fori_loop(0, 2, one, 0)

    def level(k, c):
        low = gx - k
        high = gx + k

        def part(f, c):
            @pl.when(inside(low))
            def _():
                along(low, True, f).wait_recv()

            @pl.when(inside(low) & (gx + 1 < gxn))
            def _():
                along(low, True, f).start()

            @pl.when(inside(high))
            def _():
                along(high, False, f).wait_recv()

            @pl.when(inside(high) & (gx > 0))
            def _():
                along(high, False, f).start()

            def side(i, c):
                z = gx + (2 * i - 1) * k

                @pl.when(inside(z))
                def _():
                    spread(z, f)

                return c

            lax.fori_loop(0, 2, side, 0)
            return c

        lax.fori_loop(0, 2, part, 0)

        @pl.when(k > 1)
        def _():
            back(k - 2)

        return c

    lax.fori_loop(1, gxn, level, 0)
    back(gxn - 2)
    out[...] = jnp.zeros_like(out)

    for f in range(2):
        collect(last, f)
        at = slice(f * width, (f + 1) * width)

        def final(d, c):
            c_hi, c_lo = split2(acc[f, pl.ds(pl.multiple_of(d * OCT_DEV, OCT_DEV), OCT_DEV), :])
            both = dot_nt(jnp.concatenate([c_hi, c_lo], axis=0), khi[d, :, at])
            out[...] += both[:OCT_DEV] + both[OCT_DEV:] + dot_nt(c_hi, klo[d, :, at])
            return c

        lax.fori_loop(0, DIRS, final, 0, unroll=4)

    all1.wait_send()

    def drain(z, c):
        for f in range(2):
            plane_all(z, f).wait_send()

            @pl.when((z <= gx) & (gx + 1 < gxn))
            def _():
                along(z, True, f).wait_send()

            @pl.when((z >= gx) & (gx > 0))
            def _():
                along(z, False, f).wait_send()

        return c

    lax.fori_loop(0, gxn, drain, 0)


def body(partials, partial_ids, read_lists, sources, targets, kernels):
    gxn = lax.axis_size("gx")
    gyn = lax.axis_size("gy")
    n = gxn * gyn
    width = partials.shape[1]
    per_owner = partials.shape[0] // n
    reads = read_lists.shape[1]
    per_reader = reads // n
    half = gyn * per_reader
    vmem = pl.BlockSpec(memory_space=pltpu.VMEM)
    hbm = pl.BlockSpec(memory_space=pl.ANY)
    dma = pltpu.SemaphoreType.DMA
    return pl.pallas_call(
        functools.partial(kernel, gxn, gyn, per_owner, per_reader),
        out_shape=jax.ShapeDtypeStruct((OCT_DEV, width), F32),
        in_specs=[hbm] * 6,
        out_specs=vmem,
        scratch_shapes=[
            pltpu.VMEM((n * per_owner, width), F32),
            pltpu.VMEM((gxn, 2, OCT_DEV, width // 2), F32),
            pltpu.VMEM((gxn, 2, half, width // 2), F32),
            pltpu.VMEM((2, reads, width // 2), F32),
            pltpu.VMEM((gxn, DIRS * OCT_DEV, half), BF16),
            pltpu.VMEM((gxn, DIRS * OCT_DEV, half), BF16),
            pltpu.VMEM((2, DIRS * OCT_DEV, width // 2), F32),
            pltpu.VMEM((DIRS, width, width), BF16),
            pltpu.VMEM((DIRS, width, width), BF16),
            pltpu.VMEM((2, width, width), F32),
            pltpu.VMEM((gxn, half, OCT_DEV), BF16),
            pltpu.VMEM(partial_ids.shape, jnp.int32),
            pltpu.VMEM(read_lists.shape, jnp.int32),
            pltpu.VMEM(sources.shape, jnp.int32),
            pltpu.VMEM(targets.shape, jnp.int32),
            dma, dma, dma, dma((4,)), dma((2,)),
            dma((2, 2, gxn)), dma((2, gxn)), dma((2, gxn)), dma((2, gxn)),
        ],
        compiler_params=pltpu.CompilerParams(
            collective_id=0, has_side_effects=True, vmem_limit_bytes=62 * 1024 * 1024
        ),
    )(partials, partial_ids, read_lists, sources, targets, kernels)


def solution(mesh):
    return jax.shard_map(
        body,
        mesh=mesh,
        in_specs=(
            P(("gx", "gy"), None),
            P(),
            P(),
            P(("gx", "gy"), None),
            P(("gx", "gy"), None),
            P(),
        ),
        out_specs=P(("gx", "gy"), None),
        check_vma=False,
    )
```
